32 devices in a mesh: rep: 4 (over z), fsdp: 8 (over y, x, core).
Axes of the slice: x: 2, y: 2, z: 4, core: 2. Of those that a mesh axis runs over, the one named last changes fastest.
Arguments:
- token_ids: int32 [12288], P(('rep', 'fsdp')), may hold values from 0 to 128255, as said below
- normed_inputs: bfloat16 [12288, 8192], P(('rep', 'fsdp')), may hold values from -6 to 6
- kv_cotangent: bfloat16 [12288, 1024], P(('rep', 'fsdp')), may hold values from -0.5 to 0.5
- replica_weights: bfloat16 [4, 8192, 1024], P('rep', 'fsdp'), may hold values from -6 to 6
- snapshot: bfloat16 [8192, 1024], P('fsdp'), may hold values from -6 to 6
- momentum: float32 [8192, 1024], P('fsdp', 'rep'), may hold values from -4 to 4
Outputs:
- input_grad: float32 [12288, 8192], P(('rep', 'fsdp'))
- weight_grad: float32 [4, 8192, 1024], P('rep', 'fsdp')
- new_weights: float32 [8192, 1024], P('fsdp')
- new_momentum: float32 [8192, 1024], P('fsdp', 'rep')
The draws below stay inside these ranges and needn't reach their ends.
Inputs may be any that keep to these rules, and one draw needn't show every extreme that they name: `token_ids`: 0 is the padding id; it fills the end of each device's sequence of 384 tokens, and each sequence holds 96 or more other ids.
All inputs are finite; a program needn't handle non-finite values.
Results may differ from the reference program's by a relative error of at most 0.0003.
Values may be sent and summed in bfloat16 or wider, within the bound.
A program may use at most 192 MiB of HBM per device.

```python
import jax
import jax.numpy as jnp
from jax import lax

D = 8192
VOCAB = 128256
TOK_DEV = 384
KV2 = 1024
TOKENS = 12288
N_REP = 4
N_FSDP = 8


def draw_token_ids(key, part):
    first_key, second_key = jax.random.split(jax.random.fold_in(key, 17))
    sequences = TOKENS // TOK_DEV
    lengths = jax.random.randint(first_key, (sequences, 1), TOK_DEV // 4, TOK_DEV + 1)
    values = jax.random.randint(second_key, (sequences, TOK_DEV), 1, VOCAB)
    places = jnp.arange(TOK_DEV)[None, :]
    return jnp.where(places < lengths, values, 0).reshape(TOKENS).astype(jnp.int32)


def spiked(drawn, stream_key, source, target, parts, factor):
    owner, partner = [(jnp.arange(drawn.shape[dim]) // (drawn.shape[dim] // parts)).reshape([-1 if axis == dim else 1 for axis in range(drawn.ndim)]) for dim in (source, target)]
    chosen = jax.random.permutation(stream_key, parts)[partner]
    strong = (owner == chosen) | (owner == (partner + parts // 2) % parts)
    return jnp.where(strong, factor * drawn, drawn)


def level_of(key, dims, shards, low, top_value):
    loudness = 1.0
    for axis_at, shards_of in shards:
        draws = jax.random.uniform(jax.random.fold_in(jax.random.fold_in(key, 6), axis_at), (shards_of,), jnp.float32, low / len(shards), top_value / len(shards))
        loudness = loudness * jnp.repeat(jnp.exp(draws), dims[axis_at] // shards_of).reshape((-1,) + (1,) * (len(dims) - 1 - axis_at))
    return loudness


def normal_values(own_key, dims, width, limit, cuts=(), held_as=jnp.bfloat16):
    factor_of = level_of(own_key, dims, cuts, -0.22, 0.18) if cuts else 1.0
    values = jax.random.normal(own_key, dims, jnp.float32) * width * factor_of
    return jnp.minimum(jnp.maximum(values, -limit), limit).astype(held_as)


def noise_with(rng, dims, width, limit, cuts, heavy, held_as=jnp.bfloat16):
    entries = width * jax.random.normal(rng, dims, jnp.float32)
    if cuts:
        entries = entries * level_of(rng, dims, cuts, -0.22, 0.18)
    return jnp.clip(spiked(entries, jax.random.fold_in(rng, 3), *heavy), -limit, limit).astype(held_as)


def setup_inputs(seed: int = 0) -> dict:
    keys = jax.random.split(jax.random.key(seed), 7)
    token_ids = draw_token_ids(jax.random.fold_in(keys[6], 71), 0)
    normed_inputs = noise_with(keys[1], (TOKENS, D), 1.0, 6.0, ((0, 32),), (0, 1, 32, 2.75))
    kv_cotangent = normal_values(keys[2], (TOKENS, KV2), (KV2 ** -0.5), 0.5, ((0, 32),))
    replica_weights = noise_with(keys[3], (N_REP, D, KV2), 1.0, 6.0, ((0, 4), (1, 8)), (0, 2, 4, 2.0))
    snapshot = normal_values(keys[4], (D, KV2), 1.0, 6.0, ((0, 8),))
    momentum = normal_values(keys[5], (D, KV2), 0.5, 4.0, ((0, 8), (1, 4)), jnp.float32)
    return {"token_ids": token_ids, "normed_inputs": normed_inputs, "kv_cotangent": kv_cotangent, "replica_weights": replica_weights, "snapshot": snapshot, "momentum": momentum}


outer_rate = 0.7
outer_beta = 0.9


def reference(token_ids, normed_inputs, kv_cotangent, replica_weights, snapshot, momentum):
    live_rows = (token_ids != 0).astype(jnp.bfloat16)[:, None]
    masked = kv_cotangent * live_rows
    inputs_grp = normed_inputs.reshape(N_REP, N_FSDP * TOK_DEV, D)
    cotan_grp = masked.reshape(N_REP, N_FSDP * TOK_DEV, KV2)

    def per_group(bundle):
        weights, inputs_one, cotan_one = bundle
        grad_inputs = jnp.dot(cotan_one, weights.T, preferred_element_type=jnp.float32)
        grad_weights = jnp.dot(inputs_one.T, cotan_one, preferred_element_type=jnp.float32)
        return grad_inputs, grad_weights

    grad_inputs, weight_grad = lax.map(per_group, (replica_weights, inputs_grp, cotan_grp))
    input_grad = grad_inputs.reshape(TOKENS, D)
    pseudo_grad = snapshot.astype(jnp.float32)[None] - replica_weights.astype(jnp.float32)
    outer_grad = jnp.sum(pseudo_grad, axis=0) / N_REP
    new_momentum = outer_beta * momentum + outer_grad
    new_weights = snapshot.astype(jnp.float32) - outer_rate * (outer_grad + outer_beta * new_momentum)
    return input_grad, weight_grad, new_weights, new_momentum
```

```python
import functools

import jax
import jax.numpy as jnp
from jax import lax
from jax.experimental import pallas as pl
from jax.experimental.pallas import tpu as pltpu
from jax.sharding import PartitionSpec as P

outer_rate = 0.7
outer_beta = 0.9


def swap(x, axis, mask):
    n = lax.axis_size(axis)
    return lax.ppermute(x, axis, [(i, i ^ mask) for i in range(n)])


def gather_by_mask(x, axis):
    n = lax.axis_size(axis)
    hi = n // 2
    lows = list(range(2, hi, 2))
    rows = x.shape[0]
    half = rows // 2
    got = {0: x}
    for m in [hi] + lows:
        got[m] = swap(x, axis, m)
    for m in lows:
        top = swap(got[hi][:half], axis, m)
        bottom = swap(got[m][half:], axis, hi)
        got[m + hi] = (top, bottom)
    for m in sorted(got):
        if isinstance(got[m], tuple):
            got[m + 1] = tuple(swap(p, axis, 1) for p in got[m])
        else:
            got[m + 1] = swap(got[m], axis, 1)
    return got


def parts_of(v):
    return v if isinstance(v, tuple) else (v,)


def dx_body(count, index, cot, *refs):
    out = refs[-1]
    weights = refs[:count]
    at = 0
    for w in weights:
        rows = w.shape[0]
        out[:, at:at + rows] = lax.dot_general(
            cot[...], w[...], (((1,), (1,)), ((), ())), preferred_element_type=jnp.float32
        )
        at += rows


def dx_block(prev, cot, weights, block, model):
    tokens, feats = cot.shape
    rest = [] if prev is None else [prev]
    width = sum(w.shape[0] for w in weights)
    grid_spec = pltpu.PrefetchScalarGridSpec(
        num_scalar_prefetch=1,
        grid=(1,),
        in_specs=[pl.BlockSpec((tokens, feats), lambda i, b: (0, 0))]
        + [pl.BlockSpec(w.shape, lambda i, b: (0, 0)) for w in weights]
        + [pl.BlockSpec(memory_space=pl.ANY) for _ in rest],
        out_specs=pl.BlockSpec((tokens, width), lambda i, b: (0, b[0])),
    )
    return pl.pallas_call(
        functools.partial(dx_body, len(weights)),
        grid_spec=grid_spec,
        out_shape=jax.ShapeDtypeStruct((tokens, model), jnp.float32),
        input_output_aliases={2 + len(weights): 0} if rest else {},
        cost_estimate=pl.CostEstimate(
            flops=2 * tokens * feats * width, bytes_accessed=6 * tokens * width, transcendentals=0
        ),
        compiler_params=pltpu.CompilerParams(vmem_limit_bytes=24 << 20),
    )(block, cot, *weights, *rest)


def dw_body(count, has_prev, *refs):
    out = refs[-1]
    total = None
    at = 0
    xs = refs[:count]
    cots = refs[count:-2] if has_prev else refs[count:-1]
    cs = []
    it = iter(cots)
    for x in xs:
        need = x.shape[0]
        pieces = []
        while need:
            c = next(it)
            pieces.append(c)
            need -= c.shape[0]
        cs.append(pieces)
    total = refs[-2][...] if has_prev else None
    for x, pieces in zip(xs, cs):
        at = 0
        for c in pieces:
            rows = c.shape[0]
            part = lax.dot_general(
                x[at:at + rows, :], c[...], (((0,), (0,)), ((), ())),
                preferred_element_type=jnp.float32,
            )
            total = part if total is None else total + part
            at += rows
    out[...] = total


def dw_block(prev, xs, cots):
    cots = [p for c in cots for p in parts_of(c)]
    tokens, rows = xs[0].shape
    feats = cots[0].shape[1]
    tile = min(rows, 256)
    specs = [pl.BlockSpec((tokens, tile), lambda i: (0, i)) for _ in xs]
    specs += [pl.BlockSpec(c.shape, lambda i: (0, 0)) for c in cots]
    args = list(xs) + cots
    aliases = {}
    if prev is not None:
        specs.append(pl.BlockSpec((tile, feats), lambda i: (i, 0)))
        aliases = {len(args): 0}
        args.append(prev)
    return pl.pallas_call(
        functools.partial(dw_body, len(xs), prev is not None),
        grid=(rows // tile,),
        in_specs=specs,
        out_specs=pl.BlockSpec((tile, feats), lambda i: (i, 0)),
        out_shape=jax.ShapeDtypeStruct((rows, feats), jnp.float32),
        input_output_aliases=aliases,
        cost_estimate=pl.CostEstimate(
            flops=2 * tokens * rows * feats * len(xs), bytes_accessed=8 * rows * feats, transcendentals=0
        ),
        compiler_params=pltpu.CompilerParams(vmem_limit_bytes=32 << 20),
    )(*args)


def per_device(token_ids, normed_inputs, kv_cotangent, replica_weights, snapshot, momentum):
    fsdp = lax.axis_size("fsdp")
    groups = lax.axis_size("rep")
    me = lax.axis_index("fsdp")
    my_rep = lax.axis_index("rep")
    weights = replica_weights[0]
    rows, feats = weights.shape
    tokens, model = normed_inputs.shape
    col_width = momentum.shape[1]

    live_rows = (token_ids != 0).astype(jnp.bfloat16)[:, None]
    masked = kv_cotangent * live_rows

    def columns(a, r):
        return lax.dynamic_slice_in_dim(a, r * col_width, col_width, 1)

    snap_part = columns(snapshot, my_rep).astype(jnp.float32)
    pseudo = snap_part - columns(weights, my_rep).astype(jnp.float32)
    for m in range(1, groups):
        pseudo = pseudo + (snap_part - swap(columns(weights, my_rep ^ m), "rep", m).astype(jnp.float32))
    outer_grad = pseudo / groups
    new_momentum = outer_beta * momentum + outer_grad
    new_part = snap_part - outer_rate * (outer_grad + outer_beta * new_momentum)
    new_weights = jnp.zeros((rows, feats), jnp.float32)
    for m in range(groups):
        part = swap(new_part, "rep", m) if m else new_part
        new_weights = lax.dynamic_update_slice_in_dim(new_weights, part, (my_rep ^ m) * col_width, 1)

    cots = gather_by_mask(masked, "fsdp")
    gathered = gather_by_mask(weights, "fsdp")

    weight_grad = None
    for m in range(0, fsdp, 2):
        xs = []
        for k in (m, m + 1):
            x = lax.dynamic_slice_in_dim(normed_inputs, (me ^ k) * rows, rows, 1)
            xs.append(swap(x, "fsdp", k) if k else x)
        weight_grad = dw_block(weight_grad, xs, [cots[m], cots[m + 1]])

    input_grad = None
    for m in range(fsdp):
        block = jnp.reshape(me ^ m, (1,)).astype(jnp.int32)
        input_grad = dx_block(input_grad, masked, parts_of(gathered[m]), block, model)

    return (input_grad, weight_grad[None], new_weights, new_momentum)


def solution(mesh):
    return jax.shard_map(
        per_device,
        mesh=mesh,
        in_specs=(
            P(("rep", "fsdp")),
            P(("rep", "fsdp"), None),
            P(("rep", "fsdp"), None),
            P("rep", "fsdp", None),
            P("fsdp", None),
            P("fsdp", "rep"),
        ),
        out_specs=(
            P(("rep", "fsdp"), None),
            P("rep", "fsdp", None),
            P("fsdp", None),
            P("fsdp", "rep"),
        ),
        check_vma=False,
    )
```

```python
import functools

import jax
import jax.numpy as jnp
from jax import lax
from jax.experimental import pallas as pl
from jax.experimental.pallas import tpu as pltpu
from jax.sharding import PartitionSpec as P

outer_rate = 0.7
outer_beta = 0.9
token_shape = jax.ShapeDtypeStruct((8, 128), jnp.float32)


def swap(x, axis, mask):
    n = lax.axis_size(axis)
    return lax.ppermute(x, axis, [(i, i ^ mask) for i in range(n)])


def send_direct(x, axis):
    n = lax.axis_size(axis)
    return {m: swap(x, axis, m) for m in [n // 2] + list(range(2, n // 2, 2))}


def relay(x, direct, axis):
    n = lax.axis_size(axis)
    hi = n // 2
    half = x.shape[0] // 2
    got = {0: x, **direct}
    for m in range(2, hi, 2):
        got[m + hi] = (swap(direct[hi][:half], axis, m), swap(direct[m][half:], axis, hi))
    for m in sorted(got):
        got[m + 1] = (
            tuple(swap(p, axis, 1) for p in got[m]) if isinstance(got[m], tuple) else swap(got[m], axis, 1)
        )
    return got


def parts_of(v):
    return v if isinstance(v, tuple) else (v,)


def dx_body(count, index, cot, *refs):
    out, token = refs[-2:]
    token[...] = jnp.zeros_like(token)
    weights = refs[:count]
    at = 0
    for w in weights:
        rows = w.shape[0]
        out[:, at:at + rows] = lax.dot_general(
            cot[...], w[...], (((1,), (1,)), ((), ())), preferred_element_type=jnp.float32
        )
        at += rows


def dx_block(prev, cot, weights, block, model, after):
    tokens, feats = cot.shape
    rest = ([] if prev is None else [prev]) + after
    width = sum(w.shape[0] for w in weights)
    grid_spec = pltpu.PrefetchScalarGridSpec(
        num_scalar_prefetch=1,
        grid=(1,),
        in_specs=[pl.BlockSpec((tokens, feats), lambda i, b: (0, 0))]
        + [pl.BlockSpec(w.shape, lambda i, b: (0, 0)) for w in weights]
        + [pl.BlockSpec(memory_space=pl.ANY) for _ in rest],
        out_specs=(pl.BlockSpec((tokens, width), lambda i, b: (0, b[0])), pl.BlockSpec((8, 128), lambda i, b: (0, 0))),
    )
    return pl.pallas_call(
        functools.partial(dx_body, len(weights)),
        grid_spec=grid_spec,
        out_shape=(jax.ShapeDtypeStruct((tokens, model), jnp.float32), token_shape),
        input_output_aliases={} if prev is None else {2 + len(weights): 0},
        cost_estimate=pl.CostEstimate(
            flops=2 * tokens * feats * width, bytes_accessed=6 * tokens * width, transcendentals=0
        ),
        compiler_params=pltpu.CompilerParams(vmem_limit_bytes=24 << 20),
    )(block, cot, *weights, *rest)


def dw_body(count, n_cots, has_prev, *refs):
    out, token = refs[-2:]
    token[...] = jnp.zeros_like(token)
    xs = refs[:count]
    cots = refs[count:count + n_cots]
    cs = []
    it = iter(cots)
    for x in xs:
        need = x.shape[0]
        pieces = []
        while need:
            c = next(it)
            pieces.append(c)
            need -= c.shape[0]
        cs.append(pieces)
    total = refs[count + n_cots][...] if has_prev else None
    for x, pieces in zip(xs, cs):
        at = 0
        for c in pieces:
            rows = c.shape[0]
            part = lax.dot_general(
                x[at:at + rows, :], c[...], (((0,), (0,)), ((), ())),
                preferred_element_type=jnp.float32,
            )
            total = part if total is None else total + part
            at += rows
    out[...] = total


def dw_block(prev, xs, cots, after):
    cots = [p for c in cots for p in parts_of(c)]
    tokens, rows = xs[0].shape
    feats = cots[0].shape[1]
    tile = min(rows, 256)
    specs = [pl.BlockSpec((tokens, tile), lambda i: (0, i)) for _ in xs]
    specs += [pl.BlockSpec(c.shape, lambda i: (0, 0)) for c in cots]
    args = list(xs) + cots
    aliases = {}
    if prev is not None:
        specs.append(pl.BlockSpec((tile, feats), lambda i: (i, 0)))
        aliases = {len(args): 0}
        args.append(prev)
    specs += [pl.BlockSpec(memory_space=pl.ANY) for _ in after]
    args += after
    return pl.pallas_call(
        functools.partial(dw_body, len(xs), len(cots), prev is not None),
        grid=(rows // tile,),
        in_specs=specs,
        out_specs=(pl.BlockSpec((tile, feats), lambda i: (i, 0)), pl.BlockSpec((8, 128), lambda i: (0, 0))),
        out_shape=(jax.ShapeDtypeStruct((rows, feats), jnp.float32), token_shape),
        input_output_aliases=aliases,
        cost_estimate=pl.CostEstimate(
            flops=2 * tokens * rows * feats * len(xs), bytes_accessed=8 * rows * feats, transcendentals=0
        ),
        compiler_params=pltpu.CompilerParams(vmem_limit_bytes=32 << 20),
    )(*args)


def assemble_body(count, slots, *refs):
    out, token = refs[-2:]
    token[...] = jnp.zeros_like(token)
    for m in range(count):
        @pl.when(pl.program_id(0) == m)
        def _():
            out[...] = refs[m][...]


def assemble(slots, parts, after):
    rows, width = parts[0].shape
    count = len(parts)
    grid_spec = pltpu.PrefetchScalarGridSpec(
        num_scalar_prefetch=1,
        grid=(count,),
        in_specs=[pl.BlockSpec((rows, width), lambda i, b: (0, 0)) for _ in parts]
        + [pl.BlockSpec(memory_space=pl.ANY) for _ in after],
        out_specs=(pl.BlockSpec((rows, width), lambda i, b: (0, b[i])), pl.BlockSpec((8, 128), lambda i, b: (0, 0))),
    )
    return pl.pallas_call(
        functools.partial(assemble_body, count),
        grid_spec=grid_spec,
        out_shape=(jax.ShapeDtypeStruct((rows, width * count), jnp.float32), token_shape),
        cost_estimate=pl.CostEstimate(flops=0, bytes_accessed=8 * rows * width * count, transcendentals=0),
        compiler_params=pltpu.CompilerParams(vmem_limit_bytes=32 << 20),
    )(slots, *parts, *after)


def per_device(token_ids, normed_inputs, kv_cotangent, replica_weights, snapshot, momentum):
    fsdp = lax.axis_size("fsdp")
    groups = lax.axis_size("rep")
    me = lax.axis_index("fsdp")
    my_rep = lax.axis_index("rep")
    weights = replica_weights[0]
    rows, feats = weights.shape
    tokens, model = normed_inputs.shape
    col_width = momentum.shape[1]

    live_rows = (token_ids != 0).astype(jnp.bfloat16)[:, None]
    masked = kv_cotangent * live_rows

    def columns(a, r):
        return lax.dynamic_slice_in_dim(a, r * col_width, col_width, 1)

    snap_part = columns(snapshot, my_rep).astype(jnp.float32)
    pseudo = snap_part - columns(weights, my_rep).astype(jnp.float32)
    for m in range(1, groups):
        pseudo = pseudo + (snap_part - swap(columns(weights, my_rep ^ m), "rep", m).astype(jnp.float32))
    outer_grad = pseudo / groups
    new_momentum = outer_beta * momentum + outer_grad
    new_part = snap_part - outer_rate * (outer_grad + outer_beta * new_momentum)
    half = fsdp // 2
    direct = [half] + list(range(2, half, 2))
    far = [m for m in range(half + 2, fsdp, 2)]

    def piece(source, k):
        return lax.dynamic_slice_in_dim(source, (me ^ k) * rows, rows, 1)

    arrived = {0: piece(normed_inputs, 0)}
    weights_near = send_direct(weights, "fsdp")
    cots_near = send_direct(masked, "fsdp")
    for k in [1] + direct + [m + 1 for m in direct]:
        arrived[k] = swap(piece(normed_inputs, k), "fsdp", k)
    far_pieces = [piece(normed_inputs, k) for m in far for k in (m, m + 1)]
    weights_near, new_part = lax.optimization_barrier((weights_near, new_part))
    new_parts = [new_part] + [swap(new_part, "rep", m) for m in range(1, groups)]
    gathered = relay(weights, weights_near, "fsdp")
    cots = relay(masked, cots_near, "fsdp")
    sent = 1 + groups // 2
    far_pieces, new_parts[1:sent] = lax.optimization_barrier((far_pieces, new_parts[1:sent]))
    for k, x in zip([k for m in far for k in (m, m + 1)], far_pieces):
        arrived[k] = swap(x, "fsdp", k)

    def dx(prev, k, after):
        block = jnp.reshape(me ^ k, (1,)).astype(jnp.int32)
        return dx_block(prev, masked, parts_of(gathered[k]), block, model, after)

    def dw(prev, ks, after):
        return dw_block(prev, [arrived[k] for k in ks], [cots[k] for k in ks], after)

    out = {"x": None, "w": None, "t": []}

    def dx(k):
        block = jnp.reshape(me ^ k, (1,)).astype(jnp.int32)
        out["x"], token = dx_block(out["x"], masked, parts_of(gathered[k]), block, model, out["t"])
        out["t"] = [token]

    def dw(*ks):
        out["w"], token = dw_block(out["w"], [arrived[k] for k in ks], [cots[k] for k in ks], out["t"])
        out["t"] = [token]

    dx(0)
    for k in direct:
        dx(k)
    dw(0, 1)
    for k in [1] + [m + 1 for m in direct]:
        dx(k)
    for m in direct:
        dw(m, m + 1)
    for m in far:
        dx(m)
        dx(m + 1)
    slots = jnp.stack([my_rep ^ m for m in range(groups)]).astype(jnp.int32)
    new_weights, token = assemble(slots, new_parts, out["t"])
    out["t"] = [token]
    for m in far:
        dw(m)
        dw(m + 1)
    input_grad, weight_grad = out["x"], out["w"]

    return (input_grad, weight_grad[None], new_weights, new_momentum)


def solution(mesh):
    return jax.shard_map(
        per_device,
        mesh=mesh,
        in_specs=(
            P(("rep", "fsdp")),
            P(("rep", "fsdp"), None),
            P(("rep", "fsdp"), None),
            P("rep", "fsdp", None),
            P("fsdp", None),
            P("fsdp", "rep"),
        ),
        out_specs=(
            P(("rep", "fsdp"), None),
            P("rep", "fsdp", None),
            P("fsdp", None),
            P("fsdp", "rep"),
        ),
        check_vma=False,
    )
```

```python
import functools

import jax
import jax.numpy as jnp
from jax import lax
from jax.experimental import pallas as pl
from jax.experimental.pallas import tpu as pltpu
from jax.sharding import PartitionSpec as P

outer_rate = 0.7
outer_beta = 0.9
token_shape = jax.ShapeDtypeStruct((8, 128), jnp.float32)


def swap(x, axis, mask):
    n = lax.axis_size(axis)
    return lax.ppermute(x, axis, [(i, i ^ mask) for i in range(n)])


def send_direct(x, axis):
    n = lax.axis_size(axis)
    return {m: swap(x, axis, m) for m in [n // 2] + list(range(2, n // 2, 2))}


def relay(x, direct, axis):
    n = lax.axis_size(axis)
    hi = n // 2
    half = x.shape[0] // 2
    got = {0: x, **direct}
    for m in range(2, hi, 2):
        got[m + hi] = (swap(direct[hi][:half], axis, m), swap(direct[m][half:], axis, hi))
    for m in sorted(got):
        got[m + 1] = (
            tuple(swap(p, axis, 1) for p in got[m]) if isinstance(got[m], tuple) else swap(got[m], axis, 1)
        )
    return got


def parts_of(v):
    return v if isinstance(v, tuple) else (v,)


def dx_body(count, index, cot, *refs):
    out, token = refs[-2:]
    token[...] = jnp.zeros_like(token)
    weights = refs[:count]
    at = 0
    for w in weights:
        rows = w.shape[0]
        out[:, at:at + rows] = lax.dot_general(
            cot[...], w[...], (((1,), (1,)), ((), ())), preferred_element_type=jnp.float32
        )
        at += rows


def dx_block(prev, cot, weights, block, model, after):
    tokens, feats = cot.shape
    rest = ([] if prev is None else [prev]) + after
    width = sum(w.shape[0] for w in weights)
    grid_spec = pltpu.PrefetchScalarGridSpec(
        num_scalar_prefetch=1,
        grid=(1,),
        in_specs=[pl.BlockSpec((tokens, feats), lambda i, b: (0, 0))]
        + [pl.BlockSpec(w.shape, lambda i, b: (0, 0)) for w in weights]
        + [pl.BlockSpec(memory_space=pl.ANY) for _ in rest],
        out_specs=(pl.BlockSpec((tokens, width), lambda i, b: (0, b[0])), pl.BlockSpec((8, 128), lambda i, b: (0, 0))),
    )
    return pl.pallas_call(
        functools.partial(dx_body, len(weights)),
        grid_spec=grid_spec,
        out_shape=(jax.ShapeDtypeStruct((tokens, model), jnp.float32), token_shape),
        input_output_aliases={} if prev is None else {2 + len(weights): 0},
        cost_estimate=pl.CostEstimate(
            flops=2 * tokens * feats * width, bytes_accessed=6 * tokens * width, transcendentals=0
        ),
        compiler_params=pltpu.CompilerParams(vmem_limit_bytes=24 << 20),
    )(block, cot, *weights, *rest)


def dw_body(count, n_cots, has_prev, *refs):
    out, token = refs[-2:]
    token[...] = jnp.zeros_like(token)
    xs = refs[:count]
    cots = refs[count:count + n_cots]
    cs = []
    it = iter(cots)
    for x in xs:
        need = x.shape[0]
        pieces = []
        while need:
            c = next(it)
            pieces.append(c)
            need -= c.shape[0]
        cs.append(pieces)
    total = refs[count + n_cots][...] if has_prev else None
    for x, pieces in zip(xs, cs):
        at = 0
        for c in pieces:
            rows = c.shape[0]
            part = lax.dot_general(
                x[at:at + rows, :], c[...], (((0,), (0,)), ((), ())),
                preferred_element_type=jnp.float32,
            )
            total = part if total is None else total + part
            at += rows
    out[...] = total


def dw_block(prev, xs, cots, after):
    cots = [p for c in cots for p in parts_of(c)]
    tokens, rows = xs[0].shape
    feats = cots[0].shape[1]
    tile = min(rows, 256)
    specs = [pl.BlockSpec((tokens, tile), lambda i: (0, i)) for _ in xs]
    specs += [pl.BlockSpec(c.shape, lambda i: (0, 0)) for c in cots]
    args = list(xs) + cots
    aliases = {}
    if prev is not None:
        specs.append(pl.BlockSpec((tile, feats), lambda i: (i, 0)))
        aliases = {len(args): 0}
        args.append(prev)
    specs += [pl.BlockSpec(memory_space=pl.ANY) for _ in after]
    args += after
    return pl.pallas_call(
        functools.partial(dw_body, len(xs), len(cots), prev is not None),
        grid=(rows // tile,),
        in_specs=specs,
        out_specs=(pl.BlockSpec((tile, feats), lambda i: (i, 0)), pl.BlockSpec((8, 128), lambda i: (0, 0))),
        out_shape=(jax.ShapeDtypeStruct((rows, feats), jnp.float32), token_shape),
        input_output_aliases=aliases,
        cost_estimate=pl.CostEstimate(
            flops=2 * tokens * rows * feats * len(xs), bytes_accessed=8 * rows * feats, transcendentals=0
        ),
        compiler_params=pltpu.CompilerParams(vmem_limit_bytes=32 << 20),
    )(*args)


def assemble_body(count, slots, *refs):
    out, token = refs[-2:]
    token[...] = jnp.zeros_like(token)
    for m in range(count):
        @pl.when(pl.program_id(0) == m)
        def _():
            out[...] = refs[m][...]


def assemble(slots, parts, after):
    rows, width = parts[0].shape
    count = len(parts)
    grid_spec = pltpu.PrefetchScalarGridSpec(
        num_scalar_prefetch=1,
        grid=(count,),
        in_specs=[pl.BlockSpec((rows, width), lambda i, b: (0, 0)) for _ in parts]
        + [pl.BlockSpec(memory_space=pl.ANY) for _ in after],
        out_specs=(pl.BlockSpec((rows, width), lambda i, b: (0, b[i])), pl.BlockSpec((8, 128), lambda i, b: (0, 0))),
    )
    return pl.pallas_call(
        functools.partial(assemble_body, count),
        grid_spec=grid_spec,
        out_shape=(jax.ShapeDtypeStruct((rows, width * count), jnp.float32), token_shape),
        cost_estimate=pl.CostEstimate(flops=0, bytes_accessed=8 * rows * width * count, transcendentals=0),
        compiler_params=pltpu.CompilerParams(vmem_limit_bytes=32 << 20),
    )(slots, *parts, *after)


def per_device(token_ids, normed_inputs, kv_cotangent, replica_weights, snapshot, momentum):
    fsdp = lax.axis_size("fsdp")
    groups = lax.axis_size("rep")
    me = lax.axis_index("fsdp")
    my_rep = lax.axis_index("rep")
    weights = replica_weights[0]
    rows, feats = weights.shape
    tokens, model = normed_inputs.shape
    col_width = momentum.shape[1]

    live_rows = (token_ids != 0).astype(jnp.bfloat16)[:, None]
    masked = kv_cotangent * live_rows

    def columns(a, r):
        return lax.dynamic_slice_in_dim(a, r * col_width, col_width, 1)

    snap_part = columns(snapshot, my_rep).astype(jnp.float32)
    pseudo = snap_part - columns(weights, my_rep).astype(jnp.float32)
    for m in range(1, groups):
        pseudo = pseudo + (snap_part - swap(columns(weights, my_rep ^ m), "rep", m).astype(jnp.float32))
    outer_grad = pseudo / groups
    new_momentum = outer_beta * momentum + outer_grad
    new_part = snap_part - outer_rate * (outer_grad + outer_beta * new_momentum)
    half = fsdp // 2
    direct = [half] + list(range(2, half, 2))
    far = [m for m in range(half + 2, fsdp, 2)]

    def piece(source, k):
        return lax.dynamic_slice_in_dim(source, (me ^ k) * rows, rows, 1)

    arrived = {0: piece(normed_inputs, 0)}
    weights_near = send_direct(weights, "fsdp")
    cots_near = send_direct(masked, "fsdp")
    for k in [1] + direct + [m + 1 for m in direct]:
        arrived[k] = swap(piece(normed_inputs, k), "fsdp", k)
    far_pieces = [piece(normed_inputs, k) for m in far for k in (m, m + 1)]
    new_parts = [new_part] + [swap(new_part, "rep", m) for m in range(1, groups)]
    gathered = relay(weights, weights_near, "fsdp")
    cots = relay(masked, cots_near, "fsdp")
    for k, x in zip([k for m in far for k in (m, m + 1)], far_pieces):
        arrived[k] = swap(x, "fsdp", k)

    def dx(prev, k, after):
        block = jnp.reshape(me ^ k, (1,)).astype(jnp.int32)
        return dx_block(prev, masked, parts_of(gathered[k]), block, model, after)

    def dw(prev, ks, after):
        return dw_block(prev, [arrived[k] for k in ks], [cots[k] for k in ks], after)

    out = {"x": None, "w": None, "t": []}

    def link(*tokens):
        out["t"] = list(tokens)

    def dx(k):
        block = jnp.reshape(me ^ k, (1,)).astype(jnp.int32)
        out["x"], token = dx_block(out["x"], masked, parts_of(gathered[k]), block, model, out["t"])
        out["t"] = []
        return token

    def dw(*ks):
        out["w"], token = dw_block(out["w"], [arrived[k] for k in ks], [cots[k] for k in ks], out["t"])
        out["t"] = []
        return token

    for m in [0] + direct[:1]:
        dw(m, m + 1)
    for k in [0] + direct + [1] + [m + 1 for m in direct]:
        dx(k)
    for m in far:
        dx(m)
        token = dx(m + 1)
    link(token)
    for m in direct[1:] + far:
        dw(m, m + 1)
    new_weights = jnp.zeros((rows, feats), jnp.float32)
    for m in range(groups):
        new_weights = lax.dynamic_update_slice_in_dim(new_weights, new_parts[m], (my_rep ^ m) * col_width, 1)
    input_grad, weight_grad = out["x"], out["w"]

    return (input_grad, weight_grad[None], new_weights, new_momentum)


def solution(mesh):
    return jax.shard_map(
        per_device,
        mesh=mesh,
        in_specs=(
            P(("rep", "fsdp")),
            P(("rep", "fsdp"), None),
            P(("rep", "fsdp"), None),
            P("rep", "fsdp", None),
            P("fsdp", None),
            P("fsdp", "rep"),
        ),
        out_specs=(
            P(("rep", "fsdp"), None),
            P("rep", "fsdp", None),
            P("fsdp", None),
            P("fsdp", "rep"),
        ),
        check_vma=False,
    )
```

```python
import functools

import jax
import jax.numpy as jnp
from jax import lax
from jax.experimental import pallas as pl
from jax.experimental.pallas import tpu as pltpu
from jax.sharding import PartitionSpec as P

outer_rate = 0.7
outer_beta = 0.9
token_shape = jax.ShapeDtypeStruct((8, 128), jnp.float32)


def swap(x, axis, mask):
    n = lax.axis_size(axis)
    return lax.ppermute(x, axis, [(i, i ^ mask) for i in range(n)])


def send_direct(x, axis):
    n = lax.axis_size(axis)
    return {m: swap(x, axis, m) for m in [n // 2] + list(range(2, n // 2, 2))}


def relay(x, direct, axis):
    n = lax.axis_size(axis)
    hi = n // 2
    half = x.shape[0] // 2
    got = {0: x, **direct}
    for m in range(2, hi, 2):
        got[m + hi] = (swap(direct[hi][:half], axis, m), swap(direct[m][half:], axis, hi))
    for m in sorted(got):
        got[m + 1] = (
            tuple(swap(p, axis, 1) for p in got[m]) if isinstance(got[m], tuple) else swap(got[m], axis, 1)
        )
    return got


def parts_of(v):
    return v if isinstance(v, tuple) else (v,)


def dx_body(count, index, cot, *refs):
    out, token = refs[-2:]
    token[...] = jnp.zeros_like(token)
    weights = refs[:count]
    at = 0
    for w in weights:
        rows = w.shape[0]
        out[:, at:at + rows] = lax.dot_general(
            cot[...], w[...], (((1,), (1,)), ((), ())), preferred_element_type=jnp.float32
        )
        at += rows


def dx_block(prev, cot, weights, block, model, after):
    tokens, feats = cot.shape
    rest = ([] if prev is None else [prev]) + after
    width = sum(w.shape[0] for w in weights)
    grid_spec = pltpu.PrefetchScalarGridSpec(
        num_scalar_prefetch=1,
        grid=(1,),
        in_specs=[pl.BlockSpec((tokens, feats), lambda i, b: (0, 0))]
        + [pl.BlockSpec(w.shape, lambda i, b: (0, 0)) for w in weights]
        + [pl.BlockSpec(memory_space=pl.ANY) for _ in rest],
        out_specs=(pl.BlockSpec((tokens, width), lambda i, b: (0, b[0])), pl.BlockSpec((8, 128), lambda i, b: (0, 0))),
    )
    return pl.pallas_call(
        functools.partial(dx_body, len(weights)),
        grid_spec=grid_spec,
        out_shape=(jax.ShapeDtypeStruct((tokens, model), jnp.float32), token_shape),
        input_output_aliases={} if prev is None else {2 + len(weights): 0},
        cost_estimate=pl.CostEstimate(
            flops=2 * tokens * feats * width, bytes_accessed=6 * tokens * width, transcendentals=0
        ),
        compiler_params=pltpu.CompilerParams(vmem_limit_bytes=24 << 20),
    )(block, cot, *weights, *rest)


def dw_body(count, n_cots, has_prev, *refs):
    out, token = refs[-2:]
    token[...] = jnp.zeros_like(token)
    xs = refs[:count]
    cots = refs[count:count + n_cots]
    cs = []
    it = iter(cots)
    for x in xs:
        need = x.shape[0]
        pieces = []
        while need:
            c = next(it)
            pieces.append(c)
            need -= c.shape[0]
        cs.append(pieces)
    total = refs[count + n_cots][...] if has_prev else None
    for x, pieces in zip(xs, cs):
        at = 0
        for c in pieces:
            rows = c.shape[0]
            part = lax.dot_general(
                x[at:at + rows, :], c[...], (((0,), (0,)), ((), ())),
                preferred_element_type=jnp.float32,
            )
            total = part if total is None else total + part
            at += rows
    out[...] = total


def dw_block(prev, xs, cots, after):
    cots = [p for c in cots for p in parts_of(c)]
    tokens, rows = xs[0].shape
    feats = cots[0].shape[1]
    tile = min(rows, 256)
    specs = [pl.BlockSpec((tokens, tile), lambda i: (0, i)) for _ in xs]
    specs += [pl.BlockSpec(c.shape, lambda i: (0, 0)) for c in cots]
    args = list(xs) + cots
    aliases = {}
    if prev is not None:
        specs.append(pl.BlockSpec((tile, feats), lambda i: (i, 0)))
        aliases = {len(args): 0}
        args.append(prev)
    specs += [pl.BlockSpec(memory_space=pl.ANY) for _ in after]
    args += after
    return pl.pallas_call(
        functools.partial(dw_body, len(xs), len(cots), prev is not None),
        grid=(rows // tile,),
        in_specs=specs,
        out_specs=(pl.BlockSpec((tile, feats), lambda i: (i, 0)), pl.BlockSpec((8, 128), lambda i: (0, 0))),
        out_shape=(jax.ShapeDtypeStruct((rows, feats), jnp.float32), token_shape),
        input_output_aliases=aliases,
        cost_estimate=pl.CostEstimate(
            flops=2 * tokens * rows * feats * len(xs), bytes_accessed=8 * rows * feats, transcendentals=0
        ),
        compiler_params=pltpu.CompilerParams(vmem_limit_bytes=32 << 20),
    )(*args)


def assemble_body(count, slots, *refs):
    out, token = refs[-2:]
    token[...] = jnp.zeros_like(token)
    for m in range(count):
        @pl.when(pl.program_id(0) == m)
        def _():
            out[...] = refs[m][...]


def assemble(slots, parts, after):
    rows, width = parts[0].shape
    count = len(parts)
    grid_spec = pltpu.PrefetchScalarGridSpec(
        num_scalar_prefetch=1,
        grid=(count,),
        in_specs=[pl.BlockSpec((rows, width), lambda i, b: (0, 0)) for _ in parts]
        + [pl.BlockSpec(memory_space=pl.ANY) for _ in after],
        out_specs=(pl.BlockSpec((rows, width), lambda i, b: (0, b[i])), pl.BlockSpec((8, 128), lambda i, b: (0, 0))),
    )
    return pl.pallas_call(
        functools.partial(assemble_body, count),
        grid_spec=grid_spec,
        out_shape=(jax.ShapeDtypeStruct((rows, width * count), jnp.float32), token_shape),
        cost_estimate=pl.CostEstimate(flops=0, bytes_accessed=8 * rows * width * count, transcendentals=0),
        compiler_params=pltpu.CompilerParams(vmem_limit_bytes=32 << 20),
    )(slots, *parts, *after)


def per_device(token_ids, normed_inputs, kv_cotangent, replica_weights, snapshot, momentum):
    fsdp = lax.axis_size("fsdp")
    groups = lax.axis_size("rep")
    me = lax.axis_index("fsdp")
    my_rep = lax.axis_index("rep")
    weights = replica_weights[0]
    rows, feats = weights.shape
    tokens, model = normed_inputs.shape
    col_width = momentum.shape[1]

    live_rows = (token_ids != 0).astype(jnp.bfloat16)[:, None]
    masked = kv_cotangent * live_rows

    def columns(a, r):
        return lax.dynamic_slice_in_dim(a, r * col_width, col_width, 1)

    snap_part = columns(snapshot, my_rep).astype(jnp.float32)
    pseudo = snap_part - columns(weights, my_rep).astype(jnp.float32)
    for m in range(1, groups):
        pseudo = pseudo + (snap_part - swap(columns(weights, my_rep ^ m), "rep", m).astype(jnp.float32))
    outer_grad = pseudo / groups
    new_momentum = outer_beta * momentum + outer_grad
    new_part = snap_part - outer_rate * (outer_grad + outer_beta * new_momentum)
    half = fsdp // 2
    direct = [half] + list(range(2, half, 2))
    far = [m for m in range(half + 2, fsdp, 2)]

    def piece(source, k):
        return lax.dynamic_slice_in_dim(source, (me ^ k) * rows, rows, 1)

    arrived = {0: piece(normed_inputs, 0)}
    weights_near = send_direct(weights, "fsdp")
    cots_near = send_direct(masked, "fsdp")
    for k in [1] + direct + [m + 1 for m in direct]:
        arrived[k] = swap(piece(normed_inputs, k), "fsdp", k)
    far_pieces = [piece(normed_inputs, k) for m in far for k in (m, m + 1)]
    new_parts = [new_part] + [swap(new_part, "rep", m) for m in range(1, groups)]
    gathered = relay(weights, weights_near, "fsdp")
    cots = relay(masked, cots_near, "fsdp")
    for k, x in zip([k for m in far for k in (m, m + 1)], far_pieces):
        arrived[k] = swap(x, "fsdp", k)

    def dx(prev, k, after):
        block = jnp.reshape(me ^ k, (1,)).astype(jnp.int32)
        return dx_block(prev, masked, parts_of(gathered[k]), block, model, after)

    def dw(prev, ks, after):
        return dw_block(prev, [arrived[k] for k in ks], [cots[k] for k in ks], after)

    out = {"x": None, "w": None, "t": []}

    def link(*tokens):
        out["t"] = list(tokens)

    def dx(k):
        block = jnp.reshape(me ^ k, (1,)).astype(jnp.int32)
        out["x"], token = dx_block(out["x"], masked, parts_of(gathered[k]), block, model, out["t"])
        out["t"] = []
        return token

    def dw(*ks):
        out["w"], token = dw_block(out["w"], [arrived[k] for k in ks], [cots[k] for k in ks], out["t"])
        out["t"] = []
        return token

    for m in [0] + direct[:1]:
        dw(m, m + 1)
    for k in [0] + direct + [1] + [m + 1 for m in direct]:
        dx(k)
    for m in far:
        dx(m)
        token = dx(m + 1)
    last_token = token
    link(token)
    for m in direct[1:] + far:
        dw(m, m + 1)
    new_parts[-1], _ = lax.optimization_barrier((new_parts[-1], last_token))
    new_weights = jnp.zeros((rows, feats), jnp.float32)
    for m in range(groups):
        new_weights = lax.dynamic_update_slice_in_dim(new_weights, new_parts[m], (my_rep ^ m) * col_width, 1)
    input_grad, weight_grad = out["x"], out["w"]

    return (input_grad, weight_grad[None], new_weights, new_momentum)


def solution(mesh):
    return jax.shard_map(
        per_device,
        mesh=mesh,
        in_specs=(
            P(("rep", "fsdp")),
            P(("rep", "fsdp"), None),
            P(("rep", "fsdp"), None),
            P("rep", "fsdp", None),
            P("fsdp", None),
            P("fsdp", "rep"),
        ),
        out_specs=(
            P(("rep", "fsdp"), None),
            P("rep", "fsdp", None),
            P("fsdp", None),
            P("fsdp", "rep"),
        ),
        check_vma=False,
    )
```
